128 devices in a mesh: dp: 4 (over x), fsdp: 4 (over z), ctx: 8 (over y, core).
Axes of the slice: x: 4, y: 4, z: 4, core: 2. Of those that a mesh axis runs over, the one named last changes fastest.
Arguments:
- tokens: bfloat16 [16, 3072, 1024], P(('dp', 'fsdp'), 'ctx'), may hold values from -24 to 24
- w_query: bfloat16 [1024, 1024], P(('fsdp', 'ctx'))
- w_key: bfloat16 [1024, 1024], P(('fsdp', 'ctx'))
- w_value: bfloat16 [1024, 1024], P(('fsdp', 'ctx')), may hold values from -0.1875 to 0.1875
- w_output: bfloat16 [1024, 1024], P(('fsdp', 'ctx')), may hold values from -0.1875 to 0.1875
- grad_out: bfloat16 [16, 3072, 1024], P(('dp', 'fsdp'), 'ctx'), may hold values from -6 to 6
- doc_lengths: int32 [16, 8], P(('dp', 'fsdp')), may hold values from 1 to 1536, 3072 in all within a row
- block_ids: int32 [16, 24, 8], replicated, may hold values from 0 to 23, as said below
Outputs:
- layer_out: bfloat16 [16, 3072, 1024], P(('dp', 'fsdp'), 'ctx')
- grad_tokens: bfloat16 [16, 3072, 1024], P(('dp', 'fsdp'), 'ctx')
- grad_w_query: float32 [1024, 1024], P(('fsdp', 'ctx'))
- grad_w_key: float32 [1024, 1024], P(('fsdp', 'ctx'))
- grad_w_value: float32 [1024, 1024], P(('fsdp', 'ctx'))
- grad_w_output: float32 [1024, 1024], P(('fsdp', 'ctx'))
The draws below stay inside these ranges and needn't reach their ends.
Inputs may be any that keep to these rules, and one draw needn't show every extreme that they name: `doc_lengths`: each row holds 8 lengths that sum to 3072; the largest is exactly 1536. `block_ids`: for head h and query block j, entries 0, 1, 2 are j - 1, j, j + 1 modulo 24, entry 3 is 0, and the other 4 entries are drawn at random; entries may repeat.
All inputs are finite; a program needn't handle non-finite values.
Results may differ from the reference program's by a relative error of at most 0.039.
Values may be sent and summed in bfloat16 or wider, within the bound.
No kernel may reach another device: no remote copies, remote signals or barrier semaphores. Data moves between devices by JAX's collectives and lax.ppermute only.
A program may use at most 128 MiB of HBM per device.

```python
import math
import jax
import jax.numpy as jnp
import numpy as np
from jax import lax

D = 1024
HEADS = 16
HEAD_DIM = 64
BLOCK = 128
NSEL = 8
NDOCS = 8
SEQ = 3072
NB = 24
SEQS = 16
TOTAL = 49152


def weight_matrix(key):
    normal = jnp.clip(jax.random.normal(key, (D, D), jnp.float32), -6.0, 6.0)
    return normal * D ** (-0.5)


def draw_w_query(key, part):
    return weight_matrix(jax.random.fold_in(key, 11)).astype(jnp.bfloat16)


def draw_w_key(key, part):
    mixed = weight_matrix(jax.random.fold_in(key, 12))
    return mixed.astype(jnp.bfloat16)


def draw_tokens(key, part):
    shape = (SEQS, SEQ, D)
    mixed = jax.random.normal(jax.random.fold_in(key, 21), shape, jnp.float32)
    return jnp.clip(mixed, -24.0, 24.0).astype(jnp.bfloat16)


def draw_block_ids(key, part):
    positions = lax.broadcasted_iota(jnp.int32, (HEADS, NB, 1), 1)
    window = jnp.concatenate([(positions + NB - 1) % NB, positions, (positions + 1) % NB, jnp.zeros_like(positions)], axis=2)
    drawn_ids = jax.random.randint(jax.random.fold_in(key, 31), (HEADS, NB, NSEL - 4), 0, NB)
    return jnp.concatenate([window, drawn_ids.astype(jnp.int32)], axis=2)


def shard_levels(key, shape, shards, least, high):
    factor_of = 1.0
    for dim, shards_of in shards:
        heights = jax.random.uniform(jax.random.fold_in(jax.random.fold_in(key, 6), dim), (shards_of,), jnp.float32, least / len(shards), high / len(shards))
        factor_of = factor_of * jnp.repeat(jnp.exp(heights), shape[dim] // shards_of).reshape((-1,) + (1,) * (len(shape) - 1 - dim))
    return factor_of


def profile(count, total, bound, lean):
    loads = [(1 << 20) // math.isqrt(standing ** lean) + 1 for standing in range(2, count + 1)]
    rest, holding = total - bound - (count - 1), [1] * (count - 1)
    while rest > 0:
        movable = [i for i in range(count - 1) if holding[i] < bound]
        pool, remaining = sum([loads[i] for i in movable]), rest
        for i in movable:
            more = min(bound - holding[i], max(1, remaining * loads[i] // pool), rest)
            holding[i] = holding[i] + more
            rest = rest - more
    return np.array([bound] + holding)


def ragged_sizes(key, count, total, bound, skew):
    if count == 2:
        one = jax.random.randint(key, (), max(1, total - bound), min(bound, total - 1) + 1)
        return jnp.stack([one, total - one])
    tallies = jnp.asarray(profile(count, total, bound, skew), jnp.int32)
    twos = (count - 1) // 2
    giver, receiver = tallies[1:1 + 2 * twos:2], tallies[2:2 + 2 * twos:2]
    margin = jnp.minimum(giver - 1, bound - receiver)
    moved = jax.random.randint(jax.random.fold_in(key, 1), (twos,), 0, 1 << 20) % (margin + 1)
    tallies = tallies.at[1:1 + 2 * twos:2].set(giver - moved).at[2:2 + 2 * twos:2].set(receiver + moved)
    return tallies[jax.random.permutation(jax.random.fold_in(key, 2), count)]


def scatter_about(own_key, shape, scale, limit, cuts=(), held_as=jnp.bfloat16):
    array = scale * jax.random.normal(own_key, shape, jnp.float32)
    if cuts:
        array = array * shard_levels(own_key, shape, cuts, -0.22, 0.18)
    return jnp.clip(array, -limit, limit).astype(held_as)


def setup_inputs(seed: int = 0) -> dict:
    arg_keys = jax.random.split(jax.random.key(seed), 9)
    tokens = draw_tokens(jax.random.fold_in(arg_keys[8], 71), 0)
    w_query = draw_w_query(jax.random.fold_in(arg_keys[8], 71), 0)
    w_key = draw_w_key(jax.random.fold_in(arg_keys[8], 71), 0)
    w_value = scatter_about(arg_keys[3], (D, D), D ** -0.5, 0.1875, ((0, 32),))
    w_output = scatter_about(arg_keys[4], (D, D), D ** -0.5, 0.1875, ((0, 32),))
    grad_out = scatter_about(arg_keys[5], (SEQS, SEQ, D), 1.0, 6.0, ((0, 16), (1, 8)))
    doc_lengths = jax.vmap(lambda own: ragged_sizes(own, NDOCS, SEQ, SEQ // 2, 2))(jax.random.split(arg_keys[6], SEQS)).reshape((SEQS, NDOCS)).astype(jnp.int32)
    block_ids = draw_block_ids(jax.random.fold_in(arg_keys[8], 71), 0)
    return dict(tokens=tokens, w_query=w_query, w_key=w_key, w_value=w_value, w_output=w_output, grad_out=grad_out, doc_lengths=doc_lengths, block_ids=block_ids)


def segment_ids(lengths, count):
    doc_ends = jnp.cumsum(lengths)
    places = jnp.arange(count, dtype=jnp.int32)
    return jnp.sum((places[None, :] >= doc_ends[:, None]).astype(jnp.int32), axis=0)


def rounded(matrix):
    return lax.optimization_barrier(matrix.astype(jnp.bfloat16)).astype(jnp.float32)


def head_pass(head_item, segments):
    queries, keys_in, values_in, grads_in, blocks = head_item
    scale_factor = HEAD_DIM ** -0.5
    flat_ids = blocks.reshape(-1)
    query_blocks = queries.reshape(NB, BLOCK, HEAD_DIM).astype(jnp.float32)
    key_blocks = keys_in.reshape(NB, BLOCK, HEAD_DIM)[flat_ids].reshape(NB, NSEL * BLOCK, HEAD_DIM).astype(jnp.float32)
    value_blocks = values_in.reshape(NB, BLOCK, HEAD_DIM)[flat_ids].reshape(NB, NSEL * BLOCK, HEAD_DIM).astype(jnp.float32)
    grad_blocks = grads_in.reshape(NB, BLOCK, HEAD_DIM).astype(jnp.float32)
    query_segs = segments.reshape(NB, BLOCK)
    key_segs = segments.reshape(NB, BLOCK)[flat_ids].reshape(NB, NSEL * BLOCK)
    live_mask = query_segs[:, :, None] == key_segs[:, None, :]
    scores = jnp.einsum("nqd,nkd->nqk", query_blocks, key_blocks) * scale_factor
    scores = jnp.where(live_mask, scores, -1e30)
    top_score = jnp.max(scores, axis=2, keepdims=True)
    weights = jnp.where(live_mask, jnp.exp(scores - top_score), 0.0)
    soft_probs = weights / jnp.sum(weights, axis=2, keepdims=True)
    probs_bf = rounded(soft_probs)
    attended = jnp.einsum("nqk,nkd->nqd", probs_bf, value_blocks).astype(jnp.bfloat16)
    row_delta = jnp.sum(grad_blocks * attended.astype(jnp.float32), axis=2, keepdims=True)
    d_probs = jnp.einsum("nqd,nkd->nqk", grad_blocks, value_blocks)
    d_scores = rounded(soft_probs * (d_probs - row_delta) * scale_factor)
    d_queries = jnp.einsum("nqk,nkd->nqd", d_scores, key_blocks).astype(jnp.bfloat16)
    key_terms = jnp.einsum("nqk,nqd->nkd", d_scores, query_blocks).reshape(NB * NSEL, BLOCK * HEAD_DIM)
    value_terms = jnp.einsum("nqk,nqd->nkd", probs_bf, grad_blocks).reshape(NB * NSEL, BLOCK * HEAD_DIM)
    d_keys = jax.ops.segment_sum(key_terms, flat_ids, num_segments=NB).astype(jnp.bfloat16)
    d_values = jax.ops.segment_sum(value_terms, flat_ids, num_segments=NB).astype(jnp.bfloat16)
    return (attended.reshape(SEQ, HEAD_DIM), d_queries.reshape(SEQ, HEAD_DIM),
            d_keys.reshape(SEQ, HEAD_DIM), d_values.reshape(SEQ, HEAD_DIM))


def split_heads(matrix):
    return matrix.reshape(SEQ, HEADS, HEAD_DIM).transpose(1, 0, 2)


def join_heads(matrix):
    return matrix.transpose(1, 0, 2).reshape(SEQ, D)


def reference(tokens, w_query, w_key, w_value, w_output, grad_out, doc_lengths, block_ids):
    def one_sequence(totals, inputs):
        tok_rows, cotangent, lengths = inputs
        segments = segment_ids(lengths, SEQ)
        queries = jnp.dot(tok_rows, w_query, preferred_element_type=jnp.float32).astype(jnp.bfloat16)
        keys_all = jnp.dot(tok_rows, w_key, preferred_element_type=jnp.float32).astype(jnp.bfloat16)
        values_all = jnp.dot(tok_rows, w_value, preferred_element_type=jnp.float32).astype(jnp.bfloat16)
        d_attended = jnp.dot(cotangent, w_output.T, preferred_element_type=jnp.float32).astype(jnp.bfloat16)

        def per_head(head_item):
            return head_pass(head_item, segments)

        results = lax.map(per_head, (split_heads(queries), split_heads(keys_all), split_heads(values_all),
                                     split_heads(d_attended), block_ids))
        attended = join_heads(results[0])
        d_queries = join_heads(results[1])
        d_keys = join_heads(results[2])
        d_values = join_heads(results[3])
        layer_out = (tok_rows.astype(jnp.float32)
                     + jnp.dot(attended, w_output, preferred_element_type=jnp.float32)).astype(jnp.bfloat16)
        grad_tokens = (cotangent.astype(jnp.float32)
                       + jnp.dot(d_queries, w_query.T, preferred_element_type=jnp.float32)
                       + jnp.dot(d_keys, w_key.T, preferred_element_type=jnp.float32)
                       + jnp.dot(d_values, w_value.T, preferred_element_type=jnp.float32)).astype(jnp.bfloat16)
        additions = (jnp.dot(tok_rows.T, d_queries, preferred_element_type=jnp.float32),
                     jnp.dot(tok_rows.T, d_keys, preferred_element_type=jnp.float32),
                     jnp.dot(tok_rows.T, d_values, preferred_element_type=jnp.float32),
                     jnp.dot(attended.T, cotangent, preferred_element_type=jnp.float32))
        totals = (totals[0] + additions[0], totals[1] + additions[1],
                  totals[2] + additions[2], totals[3] + additions[3])
        return totals, (layer_out, grad_tokens)

    zero_grad = jnp.zeros((D, D), jnp.float32)
    totals, outputs = lax.scan(one_sequence, (zero_grad, zero_grad, zero_grad, zero_grad),
                               (tokens, grad_out, doc_lengths))
    grad_scale = TOTAL ** -0.5
    return (outputs[0], outputs[1], totals[0] * grad_scale, totals[1] * grad_scale,
            totals[2] * grad_scale, totals[3] * grad_scale)
```

```python
import functools

import jax
import jax.numpy as jnp
from jax import lax
from jax.experimental import pallas as pl
from jax.experimental.pallas import tpu as pltpu
from jax.sharding import PartitionSpec as P

HEADS = 16
HEAD_DIM = 64
BLOCK = 128
BAND = 2 * HEAD_DIM
F32 = jnp.float32
BF16 = jnp.bfloat16


def dot_nt(left, right):
    return lax.dot_general(left, right, (((1,), (1,)), ((), ())), preferred_element_type=F32)


def dot_tn(left, right):
    return lax.dot_general(left, right, (((0,), (0,)), ((), ())), preferred_element_type=F32)


def dot_nn(left, right):
    return lax.dot_general(left, right, (((1,), (0,)), ((), ())), preferred_element_type=F32)


def attention_kernel(
    blocks_ref, ends_ref, segs_ref, q_ref, g_ref, kv0_ref, kv1_ref,
    out_ref, acc0_ref, acc1_ref, kvt0_ref, kvt1_ref, segb_ref,
    *, block_count, select, docs,
):
    seq_len = block_count * BLOCK

    def prepare(block, carry):
        rows = pl.ds(pl.multiple_of(block * BLOCK, BLOCK), BLOCK)
        place = lax.broadcasted_iota(jnp.int32, (BLOCK, BLOCK), 0) + block * BLOCK
        seg = jnp.zeros((BLOCK, BLOCK), jnp.int32)
        for doc in range(docs):
            seg = seg + (place >= ends_ref[doc]).astype(jnp.int32)
        segb_ref[rows, :] = seg
        kvt0_ref[rows, :] = kv0_ref[rows, :].T
        kvt1_ref[rows, :] = kv1_ref[rows, :].T
        acc0_ref[rows, :] = jnp.zeros((BLOCK, BAND), F32)
        acc1_ref[rows, :] = jnp.zeros((BLOCK, BAND), F32)
        return carry

    lax.fori_loop(0, block_count, prepare, 0)
    low = lax.broadcasted_iota(jnp.int32, (BLOCK, BAND), 1) < HEAD_DIM

    def one_head(head, j, q_block, g_block, seg_row):
        kv_ref, kvt_ref, acc_ref = ((kv0_ref, kvt0_ref, acc0_ref), (kv1_ref, kvt1_ref, acc1_ref))[head]
        base = (head * block_count + j) * select
        rows = []
        for slot in range(select):
            start = pl.multiple_of(blocks_ref[base + slot] * BLOCK, BLOCK)
            rows.append(pl.ds(start, BLOCK))
        zero = jnp.zeros_like(q_block)
        if head == 0:
            pair = jnp.concatenate([jnp.where(low, q_block, zero), jnp.where(low, zero, g_block)], axis=0)
        else:
            pair = jnp.concatenate([jnp.where(low, zero, q_block), jnp.where(low, g_block, zero)], axis=0)
        kv = jnp.concatenate([kv_ref[r, :] for r in rows], axis=0)
        both = dot_nt(kv, pair)
        seg_keys = jnp.concatenate([segb_ref[r, :] for r in rows], axis=0)
        scores = jnp.where(seg_keys == seg_row, both[:, :BLOCK], -jnp.inf)
        d_probs = both[:, BLOCK:]
        weights = jnp.exp(scores - jnp.max(scores, axis=0, keepdims=True))
        probs = weights * (1.0 / jnp.sum(weights, axis=0, keepdims=True))
        delta = jnp.sum(probs * d_probs, axis=0, keepdims=True)
        d_scores = probs * (d_probs - delta)
        packed = jnp.concatenate([d_scores.astype(BF16), probs.astype(BF16)], axis=1)
        terms = dot_nn(packed, pair)
        for slot in range(select):
            acc_ref[rows[slot], :] += terms[slot * BLOCK:(slot + 1) * BLOCK, :]
        kvt = jnp.concatenate([kvt_ref[r, :] for r in rows], axis=1)
        back = dot_nn(kvt, packed)
        if head == 0:
            return back[:HEAD_DIM, :BLOCK], back[HEAD_DIM:, BLOCK:]
        return back[HEAD_DIM:, :BLOCK], back[:HEAD_DIM, BLOCK:]

    def one_block(j, carry):
        rows = pl.ds(pl.multiple_of(j * BLOCK, BLOCK), BLOCK)
        q_block = q_ref[rows, :]
        g_block = g_ref[rows, :]
        seg_row = segs_ref[pl.ds(j, 1), :]
        dq0, o0 = one_head(0, j, q_block, g_block, seg_row)
        dq1, o1 = one_head(1, j, q_block, g_block, seg_row)
        out_ref[rows, 0:BAND] = jnp.concatenate([o1, o0], axis=0).T.astype(BF16)
        d_query = jnp.concatenate([dq0, dq1], axis=0) * (HEAD_DIM ** -0.5)
        out_ref[rows, BAND:2 * BAND] = d_query.T.astype(BF16)
        return carry

    lax.fori_loop(0, block_count, one_block, 0)
    out_ref[:, 2 * BAND:3 * BAND] = acc0_ref[...].astype(BF16)
    out_ref[:, 3 * BAND:4 * BAND] = acc1_ref[...].astype(BF16)


def attention(blocks, ends, segs, q_band, g_band, kv0, kv1):
    seq_len = q_band.shape[0]
    block_count = seq_len // BLOCK
    body = functools.partial(
        attention_kernel, block_count=block_count, select=blocks.shape[-1], docs=ends.shape[0]
    )
    vmem = pl.BlockSpec(memory_space=pltpu.VMEM)
    smem = pl.BlockSpec(memory_space=pltpu.SMEM)
    return pl.pallas_call(
        body,
        out_shape=jax.ShapeDtypeStruct((seq_len, 4 * BAND), BF16),
        in_specs=[smem, smem, vmem, vmem, vmem, vmem, vmem],
        out_specs=vmem,
        scratch_shapes=[
            pltpu.VMEM((seq_len, BAND), F32),
            pltpu.VMEM((seq_len, BAND), F32),
            pltpu.VMEM((seq_len, BAND), BF16),
            pltpu.VMEM((seq_len, BAND), BF16),
            pltpu.VMEM((seq_len, BLOCK), jnp.int32),
        ],
        compiler_params=pltpu.CompilerParams(vmem_limit_bytes=56 * 1024 * 1024),
        name="attention",
    )(blocks.reshape(-1), ends, segs, q_band, g_band, kv0, kv1)


def finish_kernel(d_ref, w_ref, wo_ref, tok_ref, cot_ref, layer_ref, grad_ref, lacc, gacc):
    step = pl.program_id(0)

    @pl.when(step == 0)
    def _():
        lacc[...] = tok_ref[...].astype(F32)
        gacc[...] = cot_ref[...].astype(F32)

    band = d_ref[0]
    lacc[...] += dot_nn(band[:, :BAND], wo_ref[0])
    gacc[...] += dot_nt(band[:, BAND:], w_ref[0])

    @pl.when(step == pl.num_programs(0) - 1)
    def _():
        layer_ref[...] = lacc[...].astype(BF16)
        grad_ref[...] = gacc[...].astype(BF16)


def finish(received, w_all, wo_all, tok_rows, cotangent):
    bands, tok_dev, wide = received.shape
    width = tok_rows.shape[1]
    whole = pl.BlockSpec((tok_dev, width), lambda c: (0, 0))
    return pl.pallas_call(
        finish_kernel,
        grid=(bands,),
        out_shape=(
            jax.ShapeDtypeStruct((tok_dev, width), BF16),
            jax.ShapeDtypeStruct((tok_dev, width), BF16),
        ),
        in_specs=[
            pl.BlockSpec((1, tok_dev, wide), lambda c: (c, 0, 0)),
            pl.BlockSpec((1, width, wide - BAND), lambda c: (c, 0, 0)),
            pl.BlockSpec((1, BAND, width), lambda c: (c, 0, 0)),
            whole,
            whole,
        ],
        out_specs=(whole, whole),
        scratch_shapes=[pltpu.VMEM((tok_dev, width), F32), pltpu.VMEM((tok_dev, width), F32)],
        compiler_params=pltpu.CompilerParams(vmem_limit_bytes=48 * 1024 * 1024),
        name="finish",
    )(received, w_all, wo_all, tok_rows, cotangent)


def gather_by_shift(piece, axis):
    size = lax.axis_size(axis)
    me = lax.axis_index(axis)
    parts = [piece]
    for shift in range(1, size):
        parts.append(lax.ppermute(piece, axis, [(i, (i + shift) % size) for i in range(size)]))
    stacked = jnp.stack(parts)
    order = (me - jnp.arange(size)) % size
    return stacked[order]


def per_device(tokens, w_query, w_key, w_value, w_output, grad_out, doc_lengths, block_ids):
    tok_rows = tokens[0]
    cotangent = grad_out[0]
    tok_dev, width = tok_rows.shape
    ctx_size = lax.axis_size("ctx")
    fsdp_size = lax.axis_size("fsdp")
    dp_size = lax.axis_size("dp")
    chips = ctx_size // 2
    shard = w_query.shape[0]
    ctx = lax.axis_index("ctx")
    chip = ctx // 2
    core = ctx % 2
    partner = [(i, i ^ 1) for i in range(ctx_size)]
    seq_len = tok_dev * ctx_size

    full_tok = lax.all_gather(tok_rows, "ctx", axis=0, tiled=True)
    full_cot = lax.all_gather(cotangent, "ctx", axis=0, tiled=True)

    def by_owner(weight):
        heads = weight.reshape(shard, 2, 2, chips, HEAD_DIM)
        return heads.transpose(3, 1, 0, 2, 4).reshape(ctx_size, shard, 2, HEAD_DIM)

    wq, wk, wv = by_owner(w_query), by_owner(w_key), by_owner(w_value)
    packed = jnp.concatenate(
        [wq[:, :, 0], wq[:, :, 1], wk[:, :, 0], wv[:, :, 0], wv[:, :, 1], wk[:, :, 1]], axis=2
    )
    swapped = lax.all_to_all(packed, "ctx", split_axis=0, concat_axis=0, tiled=True)
    band_w = gather_by_shift(swapped, "fsdp").reshape(width, 3 * BAND)

    halves = gather_by_shift(w_output, "fsdp").reshape(2, 2, shard, width)
    kept = lax.dynamic_index_in_dim(halves, core, 0, keepdims=False)
    taken = lax.ppermute(lax.dynamic_index_in_dim(halves, 1 - core, 0, keepdims=False), "ctx", partner)
    first_half = jnp.where(core == 0, kept, taken)
    second_half = jnp.where(core == 0, taken, kept)
    whole_heads = jnp.concatenate([first_half, second_half], axis=1)
    band_wo = jnp.concatenate([whole_heads[1], whole_heads[0]], axis=0)

    projected = dot_nn(full_tok, band_w)
    q_band = (projected[:, :BAND].astype(BF16) * (HEAD_DIM ** -0.5)).astype(BF16)
    kv0 = projected[:, BAND:2 * BAND].astype(BF16)
    kv1 = projected[:, 2 * BAND:].astype(BF16)
    g_band = dot_nt(full_cot, band_wo).astype(BF16)

    ends = jnp.cumsum(doc_lengths[0])
    places = lax.broadcasted_iota(jnp.int32, (ends.shape[0], seq_len), 1)
    segs = jnp.sum((places >= ends[:, None]).astype(jnp.int32), axis=0).reshape(-1, BLOCK)
    first = 8 * core + chip
    blocks = jnp.stack([
        lax.dynamic_index_in_dim(block_ids, first, 0, keepdims=False),
        lax.dynamic_index_in_dim(block_ids, first + chips, 0, keepdims=False),
    ])
    result = attention(blocks, ends, segs, q_band, g_band, kv0, kv1)

    w_all = lax.all_gather(band_w, "ctx", axis=0, tiled=False)
    wo_all = lax.all_gather(band_wo, "ctx", axis=0, tiled=False)
    received = lax.all_to_all(
        result.reshape(ctx_size, tok_dev, 4 * BAND), "ctx", split_axis=0, concat_axis=0, tiled=True
    )
    layer_out, grad_tokens = finish(received, w_all, wo_all, tok_rows, cotangent)

    d_w = dot_tn(full_tok, result[:, BAND:]).astype(BF16)
    d_wo = dot_tn(result[:, :BAND], full_cot).astype(BF16)
    heads = jnp.stack([d_wo[HEAD_DIM:], d_wo[:HEAD_DIM]]).reshape(2, 2, shard, width)
    keep = lax.dynamic_index_in_dim(heads, core, 1, keepdims=False)
    take = lax.ppermute(lax.dynamic_index_in_dim(heads, 1 - core, 1, keepdims=False), "ctx", partner)
    wo_rows = jnp.where(core == 0, jnp.concatenate([keep, take]), jnp.concatenate([take, keep]))
    flat = jnp.concatenate(
        [d_w.reshape(fsdp_size, -1, width), wo_rows.reshape(fsdp_size, -1, width)], axis=1
    )
    summed = jnp.sum(
        lax.all_to_all(flat, "fsdp", split_axis=0, concat_axis=0, tiled=True).astype(F32), axis=0
    ).astype(BF16)
    parts = [summed] + [
        lax.ppermute(summed, "dp", [(i, (i + s) % dp_size) for i in range(dp_size)])
        for s in range(1, dp_size)
    ]
    total = sum(part.astype(F32) for part in parts)
    total_tokens = seq_len * dp_size * fsdp_size
    total = total * (total_tokens ** -0.5)
    qkv_rows = total.shape[0] - shard
    grad_wo = total[qkv_rows:]
    rows_qkv = lax.all_to_all(
        total[:qkv_rows].reshape(ctx_size, shard, 3 * BAND), "ctx", split_axis=0, concat_axis=0, tiled=True
    )

    def in_head_order(first_head, second_head):
        both = jnp.stack([first_head, second_head], axis=2)
        both = both.reshape(chips, 2, shard, 2, HEAD_DIM)
        return both.transpose(2, 1, 3, 0, 4).reshape(shard, width)

    piece = [rows_qkv[:, :, i * HEAD_DIM:(i + 1) * HEAD_DIM] for i in range(6)]
    return (
        layer_out[None],
        grad_tokens[None],
        in_head_order(piece[0], piece[1]),
        in_head_order(piece[2], piece[5]),
        in_head_order(piece[3], piece[4]),
        grad_wo,
    )


def solution(mesh):
    in_specs = (
        P(("dp", "fsdp"), "ctx", None),
        P(("fsdp", "ctx"), None),
        P(("fsdp", "ctx"), None),
        P(("fsdp", "ctx"), None),
        P(("fsdp", "ctx"), None),
        P(("dp", "fsdp"), "ctx", None),
        P(("dp", "fsdp"), None),
        P(),
    )
    out_specs = (
        P(("dp", "fsdp"), "ctx", None),
        P(("dp", "fsdp"), "ctx", None),
        P(("fsdp", "ctx"), None),
        P(("fsdp", "ctx"), None),
        P(("fsdp", "ctx"), None),
        P(("fsdp", "ctx"), None),
    )
    return jax.shard_map(
        per_device, mesh=mesh, in_specs=in_specs, out_specs=out_specs, check_vma=False
    )
```
